32 devices in a mesh: groups: 2 (over y), seq: 4 (over z), head: 4 (over x, core).
Axes of the slice: x: 2, y: 2, z: 4, core: 2. Of those that a mesh axis runs over, the one named last changes fastest.
Arguments:
- query: bfloat16 [8192, 1536], P(('groups', 'seq', 'head')), parts along dimension 0, may hold values from -150 to 150
- key_in: bfloat16 [8192, 1536], P(('groups', 'seq', 'head')), parts along dimension 0, may hold values from -6 to 6
- value: bfloat16 [8192, 1536], P(('groups', 'seq', 'head')), parts along dimension 0, may hold values from -6 to 6
- grad_out: bfloat16 [8192, 1536], P(('groups', 'seq', 'head')), parts along dimension 0, may hold values from -6 to 6
- pattern: int32 [16, 3], replicated, may hold values from 0 to 15, as said below
- live: int32 [16, 3], replicated, may hold values from 0 to 1, as said below
Outputs:
- attended: bfloat16 [8192, 1536], P(('groups', 'seq', 'head')), parts along dimension 0
- query_grad: bfloat16 [8192, 1536], P(('groups', 'seq', 'head')), parts along dimension 0
- key_grad: bfloat16 [8192, 1536], P(('groups', 'seq', 'head')), parts along dimension 0
- value_grad: bfloat16 [8192, 1536], P(('groups', 'seq', 'head')), parts along dimension 0
The draws below stay inside these ranges and needn't reach their ends.
There are 2 independent parts, one for each index of `groups`. The reference program is written for one: setup_inputs(seed, part) draws one part's arguments, and reference() takes and returns one part's arrays. A program takes and returns all parts, laid end to end along the dimension named above; an argument that names none is the same for every part. Nothing has to cross between parts.
Inputs may be any that keep to these rules, and one draw needn't show every extreme that they name: `pattern`: each entry names a tile of the same frame-tile layer as its query tile or of the layer just before or after it; the live entries of a row are distinct; an entry that is not live names the query tile itself. Slot 0 of every row is live and names the query tile itself.
All inputs are finite; a program needn't handle non-finite values.
Results may differ from the reference program's by a relative error of at most 0.015.
Values may be sent and summed in bfloat16 or wider, within the bound.
A program may use at most 128 MiB of HBM per device.

```python
import jax
import jax.numpy as jnp
from jax import lax

HEADS = 12
HEAD_DIM = 128
TILE = 256
NB = 3
SPAN = 4
LAYERS = 4
NTILES = 16
TOKENS = 4096


def query_and_keys(key):
    shape = (TOKENS, HEADS * HEAD_DIM)
    keys = jax.random.truncated_normal(jax.random.fold_in(key, 101), -6.0, 6.0, shape, jnp.float32)
    queries = jax.random.truncated_normal(jax.random.fold_in(key, 102), -6.0, 6.0, shape, jnp.float32)
    return (queries, keys)


def draw_query(key, part):
    return query_and_keys(key)[0].astype(jnp.bfloat16)


def draw_key_in(key, part):
    return query_and_keys(key)[1].astype(jnp.bfloat16)


def neighbour_table(key):
    choices_count = 3 * SPAN
    tiles = jnp.arange(NTILES, dtype=jnp.int32)
    layer = tiles // SPAN
    spot = tiles % SPAN
    columns = jnp.arange(choices_count, dtype=jnp.int32)[None, :]
    noise = jax.random.randint(jax.random.fold_in(key, 201), (NTILES, choices_count), 0, 1 << 20)
    ranking = noise * choices_count + columns
    ranking = jnp.where(columns == (SPAN + spot)[:, None], jnp.int32(1 << 30), ranking)
    order = jnp.argsort(ranking, axis=1)[:, :NB - 1].astype(jnp.int32)
    target_layer = layer[:, None] + order // SPAN - 1
    target = target_layer * SPAN + order % SPAN
    inside = (target_layer >= 0) & (target_layer < LAYERS)
    keep = jax.random.randint(jax.random.fold_in(key, 202), (NTILES, NB - 1), 0, 4) > 0
    used = inside & keep
    table = jnp.concatenate([tiles[:, None], jnp.where(used, target, tiles[:, None])], axis=1).astype(jnp.int32)
    flags = jnp.concatenate([jnp.ones((NTILES, 1), jnp.int32), used.astype(jnp.int32)], axis=1)
    return (table, flags)


def draw_pattern(key, part):
    return neighbour_table(key)[0]


def draw_live(key, part):
    return neighbour_table(key)[1]


def block_scale(key, shape, pieces, least, top_value):
    factor_of = 1.0
    for dim, parts in pieces:
        draws = jax.random.uniform(jax.random.fold_in(jax.random.fold_in(key, 6), dim), (parts,), jnp.float32, least / len(pieces), top_value / len(pieces))
        factor_of = factor_of * jnp.repeat(jnp.exp(draws), shape[dim] // parts).reshape((-1,) + (1,) * (len(shape) - 1 - dim))
    return factor_of


def scatter_about(rng, shape, deviation, limit, shards=(), kind=jnp.bfloat16):
    gain = block_scale(rng, shape, shards, -0.22, 0.18) if shards else 1.0
    drawn = jax.random.normal(rng, shape, jnp.float32) * deviation * gain
    return jnp.minimum(jnp.maximum(drawn, -limit), limit).astype(kind)


def setup_inputs(seed: int = 0, part: int = 0) -> dict:
    key_of = jax.random.split(jax.random.key(seed), 7)
    own_keys = jax.random.split(jax.random.fold_in(key_of[6], part), 7)
    query = draw_query(jax.random.fold_in(jax.random.fold_in(key_of[6], part), 71), part)
    key_in = draw_key_in(jax.random.fold_in(jax.random.fold_in(key_of[6], part), 71), part)
    value = scatter_about(own_keys[2], (TOKENS, HEADS * HEAD_DIM), 1.0, 6.0, ((0, 16),))
    grad_out = scatter_about(own_keys[3], (TOKENS, HEADS * HEAD_DIM), 1.0, 6.0, ((0, 16),))
    pattern = draw_pattern(jax.random.fold_in(key_of[6], 71), part)
    live = draw_live(jax.random.fold_in(key_of[6], 71), part)
    return {"query": query, "key_in": key_in, "value": value, "grad_out": grad_out, "pattern": pattern, "live": live}


def reference(query, key_in, value, grad_out, pattern, live):
    width = HEADS * HEAD_DIM
    scale = HEAD_DIM ** -0.5
    queries = query.reshape(NTILES, TILE, HEADS, HEAD_DIM)
    keys = key_in.reshape(NTILES, TILE, HEADS, HEAD_DIM)
    values = value.reshape(NTILES, TILE, HEADS, HEAD_DIM)
    out_grads = grad_out.reshape(NTILES, TILE, HEADS, HEAD_DIM)

    def visit(carry, index):
        key_total, value_total = carry
        tile_ids = pattern[index].astype(jnp.int32)
        alive = live[index] > 0
        q_tile = queries[index].astype(jnp.float32)
        g_tile = out_grads[index].astype(jnp.float32)
        k_tiles = keys[tile_ids].astype(jnp.float32)
        v_tiles = values[tile_ids].astype(jnp.float32)
        scores = jnp.einsum('qhd,nkhd->hqnk', q_tile, k_tiles) * scale
        scores = jnp.where(alive[None, None, :, None], scores, -jnp.inf)
        peak = jnp.max(scores, axis=(2, 3), keepdims=True)
        exponent = jnp.exp(scores - peak)
        weights = exponent / jnp.sum(exponent, axis=(2, 3), keepdims=True)
        weights_low = lax.optimization_barrier(weights.astype(jnp.bfloat16)).astype(jnp.float32)
        attended = jnp.einsum('hqnk,nkhd->qhd', weights_low, v_tiles).astype(jnp.bfloat16)
        weight_grad = jnp.einsum('qhd,nkhd->hqnk', g_tile, v_tiles)
        delta = jnp.sum(weights * weight_grad, axis=(2, 3), keepdims=True)
        score_grad = lax.optimization_barrier((weights * (weight_grad - delta) * scale).astype(jnp.bfloat16)).astype(jnp.float32)
        query_grad = jnp.einsum('hqnk,nkhd->qhd', score_grad, k_tiles).astype(jnp.bfloat16)
        key_part = jnp.einsum('hqnk,qhd->nkhd', score_grad, q_tile)
        value_part = jnp.einsum('hqnk,qhd->nkhd', weights_low, g_tile)
        key_total = key_total.at[tile_ids].add(key_part)
        value_total = value_total.at[tile_ids].add(value_part)
        return (key_total, value_total), (attended, query_grad)

    zeros = jnp.zeros((NTILES, TILE, HEADS, HEAD_DIM), jnp.float32)
    (key_total, value_total), (attended, query_grad) = lax.scan(visit, (zeros, zeros), jnp.arange(NTILES, dtype=jnp.int32))
    return (attended.reshape(TOKENS, width), query_grad.reshape(TOKENS, width),
            key_total.astype(jnp.bfloat16).reshape(TOKENS, width), value_total.astype(jnp.bfloat16).reshape(TOKENS, width))
```

```python
import functools

import jax
import jax.numpy as jnp
from jax import lax
from jax.experimental import pallas as pl
from jax.experimental.pallas import tpu as pltpu
from jax.sharding import PartitionSpec as P

HEADS = 12
HEAD_DIM = 128
MESH = pl.DeviceIdType.MESH
NT = (((1,), (1,)), ((), ()))
NN = (((1,), (0,)), ((), ()))
TN = (((0,), (0,)), ((), ()))


def dot(a, b, dims):
    return lax.dot_general(a, b, dims, preferred_element_type=jnp.float32)


def kernel(
    members, layers, pattern, live, query, key_in, value, grad_out,
    att_out, dq_out, dk_out, dv_out,
    qg, res, slots, own, gsend, grecv, total,
    xin_send, xin_recv, xin_local, z_send, z_recv, zb_send, zb_recv,
    xb_send, xb_recv, xb_local, *kv,
):
    me = lax.axis_index("head")
    seq = lax.axis_index("seq")
    heads = HEADS // members
    nb = pattern.shape[1]
    first = seq * members
    scale = HEAD_DIM ** (-0.5)
    has_below = seq > 0
    has_above = seq < layers - 1
    below = jnp.maximum(seq - 1, 0)
    above = jnp.minimum(seq + 1, layers - 1)
    partners = [lax.rem(me + off, members) for off in range(1, members)]

    def columns(owner, h):
        return pl.ds(pl.multiple_of((owner * heads + h) * HEAD_DIM, HEAD_DIM), HEAD_DIM)

    barrier = pltpu.get_barrier_semaphore()
    for p in partners:
        pl.semaphore_signal(barrier, inc=1, device_id={"head": p}, device_id_type=MESH)

    @pl.when(has_below)
    def _():
        pl.semaphore_signal(barrier, inc=1, device_id={"seq": below}, device_id_type=MESH)

    @pl.when(has_above)
    def _():
        pl.semaphore_signal(barrier, inc=1, device_id={"seq": above}, device_id_type=MESH)

    pl.semaphore_wait(
        barrier, members - 1 + has_below.astype(jnp.int32) + has_above.astype(jnp.int32)
    )

    sources = (key_in, value, query, grad_out)

    def landing(h, arr, tile):
        if arr < 2:
            return kv[h].at[members + tile, arr]
        return qg.at[h, tile, arr - 2]

    def x_in(h, arr, off):
        return pltpu.make_async_remote_copy(
            src_ref=sources[arr].at[:, columns(partners[off], h)],
            dst_ref=landing(h, arr, me),
            send_sem=xin_send.at[h, arr, off],
            recv_sem=xin_recv.at[h, arr, off],
            device_id={"head": partners[off]},
            device_id_type=MESH,
        )

    def x_own(h, arr):
        return pltpu.make_async_copy(
            sources[arr].at[:, columns(me, h)], landing(h, arr, me), xin_local.at[h, arr]
        )

    def x_in_wait(h, arrs):
        for arr in arrs:
            x_own(h, arr).wait()
            for off in range(members - 1):
                x_in(h, arr, off).wait_recv()

    def z_in(h, up):
        return pltpu.make_async_remote_copy(
            src_ref=kv[h].at[pl.ds(members, members)],
            dst_ref=kv[h].at[pl.ds(0 if up else 2 * members, members)],
            send_sem=z_send.at[h, up],
            recv_sem=z_recv.at[h, up],
            device_id={"seq": above if up else below},
            device_id_type=MESH,
        )

    def z_back(h, up):
        return pltpu.make_async_remote_copy(
            src_ref=gsend.at[h, up],
            dst_ref=grecv.at[h, up],
            send_sem=zb_send.at[h, up],
            recv_sem=zb_recv.at[h, up],
            device_id={"seq": above if up else below},
            device_id_type=MESH,
        )

    def z_start(make, h):
        for up, there in ((1, has_above), (0, has_below)):
            @pl.when(there)
            def _():
                make(h, up).start()

    def z_wait_recv(make, h):
        for up, there in ((1, has_below), (0, has_above)):
            @pl.when(there)
            def _():
                make(h, up).wait_recv()

    def z_wait_send(make, h):
        for up, there in ((1, has_above), (0, has_below)):
            @pl.when(there)
            def _():
                make(h, up).wait_send()

    results = (dk_out, dv_out, att_out, dq_out)

    def outgoing(h, arr, tile):
        if arr < 2:
            return total.at[h, tile, arr]
        return res.at[h, tile, arr - 2]

    def x_back(h, arr, off):
        return pltpu.make_async_remote_copy(
            src_ref=outgoing(h, arr, partners[off]),
            dst_ref=results[arr].at[:, columns(me, h)],
            send_sem=xb_send.at[h, arr, off],
            recv_sem=xb_recv.at[h, arr, off],
            device_id={"head": partners[off]},
            device_id_type=MESH,
        )

    def x_back_own(h, arr):
        return pltpu.make_async_copy(
            outgoing(h, arr, me), results[arr].at[:, columns(me, h)], xb_local.at[h, arr]
        )

    def x_back_start(h, arrs):
        for arr in arrs:
            for off in range(members - 1):
                x_back(h, arr, off).start()
            x_back_own(h, arr).start()

    def attend(h):
        def tile_step(a, carry):
            row = first + a
            ids = [
                jnp.clip(pattern[row, n] - first + members, 0, 3 * members - 1) for n in range(nb)
            ]
            bias = [jnp.where(live[row, n] > 0, 0.0, -jnp.inf) for n in range(nb)]
            q = qg[h, a, 0]
            g = qg[h, a, 1]
            scores = [dot(q, kv[h][ids[n], 0], NT) * scale + bias[n] for n in range(nb)]
            peak = functools.reduce(
                jnp.maximum, [jnp.max(s, axis=1, keepdims=True) for s in scores]
            )
            exps = [jnp.exp(s - peak) for s in scores]
            norm = 1.0 / sum(jnp.sum(e, axis=1, keepdims=True) for e in exps)
            weights = [e * norm for e in exps]
            low = [w.astype(jnp.bfloat16) for w in weights]
            res[h, a, 0] = sum(dot(low[n], kv[h][ids[n], 1], NN) for n in range(nb)).astype(
                jnp.bfloat16
            )
            wgrad = [dot(g, kv[h][ids[n], 1], NT) for n in range(nb)]
            delta = sum(
                jnp.sum(weights[n] * wgrad[n], axis=1, keepdims=True) for n in range(nb)
            )
            sgrad = [
                (weights[n] * (wgrad[n] - delta) * scale).astype(jnp.bfloat16)
                for n in range(nb)
            ]
            res[h, a, 1] = sum(dot(sgrad[n], kv[h][ids[n], 0], NN) for n in range(nb)).astype(
                jnp.bfloat16
            )
            for n in range(nb):
                slots[a * nb + n, 0] = dot(sgrad[n], q, TN)
                slots[a * nb + n, 1] = dot(low[n], g, TN)
            return carry

        lax.fori_loop(0, members, tile_step, 0)

    def gather_slots(j, which):
        terms = []
        for a in range(members):
            row = first + a
            index = jnp.int32(members * nb)
            for n in range(nb):
                hit = (pattern[row, n] - first + members == j) & (live[row, n] > 0)
                index = jnp.where(hit, a * nb + n, index)
            terms.append(index)
        return sum(slots[index, which] for index in terms)

    def spread(h):
        def outer(j, carry):
            for which in range(2):
                gsend[h, 0, j, which] = gather_slots(j, which).astype(jnp.bfloat16)
                gsend[h, 1, j, which] = gather_slots(j + 2 * members, which).astype(jnp.bfloat16)
            return carry

        lax.fori_loop(0, members, outer, 0)
        z_start(z_back, h)

        def inner(j, carry):
            for which in range(2):
                own[h, j, which] = gather_slots(j + members, which)
            return carry

        lax.fori_loop(0, members, inner, 0)

    def finish(h):
        z_wait_recv(z_back, h)

        @pl.when(has_below)
        def _():
            own[h] += grecv[h, 1].astype(jnp.float32)

        @pl.when(has_above)
        def _():
            own[h] += grecv[h, 0].astype(jnp.float32)

        total[h] = own[h].astype(jnp.bfloat16)
        x_back_start(h, (0, 1))

    for h in range(heads):
        for arr in range(4):
            for off in range(members - 1):
                x_in(h, arr, off).start()
            x_own(h, arr).start()

    slots[members * nb] = jnp.zeros(slots.shape[1:], slots.dtype)

    def feed(h):
        x_in_wait(h, (0, 1))
        z_start(z_in, h)

    feed(0)
    for h in range(heads):
        if h + 1 < heads:
            feed(h + 1)
        x_in_wait(h, (2, 3))
        z_wait_recv(z_in, h)
        attend(h)
        x_back_start(h, (2, 3))
        spread(h)
        if h >= 2:
            finish(h - 2)
    for h in range(max(heads - 2, 0), heads):
        finish(h)

    for h in range(heads):
        z_wait_send(z_in, h)
        z_wait_send(z_back, h)
        for arr in range(4):
            x_back_own(h, arr).wait()
            for off in range(members - 1):
                x_in(h, arr, off).wait_send()
                x_back(h, arr, off).wait_send()
                x_back(h, arr, off).wait_recv()


def body(members, layers, query, key_in, value, grad_out, pattern, live):
    tile = query.shape[0]
    heads = HEADS // members
    nb = pattern.shape[1]
    dma = pltpu.SemaphoreType.DMA
    bf16 = jnp.bfloat16
    block = (tile, HEAD_DIM)
    return pl.pallas_call(
        functools.partial(kernel, members, layers),
        out_shape=[jax.ShapeDtypeStruct(query.shape, bf16)] * 4,
        in_specs=[pl.BlockSpec(memory_space=pltpu.SMEM)] * 2
        + [pl.BlockSpec(memory_space=pl.ANY)] * 4,
        out_specs=[pl.BlockSpec(memory_space=pl.ANY)] * 4,
        scratch_shapes=[
            pltpu.VMEM((heads, members, 2) + block, bf16),
            pltpu.VMEM((heads, members, 2) + block, bf16),
            pltpu.VMEM((members * nb + 1, 2) + block, jnp.float32),
            pltpu.VMEM((heads, members, 2) + block, jnp.float32),
            pltpu.VMEM((heads, 2, members, 2) + block, bf16),
            pltpu.VMEM((heads, 2, members, 2) + block, bf16),
            pltpu.VMEM((heads, members, 2) + block, bf16),
            dma((heads, 4, members - 1)),
            dma((heads, 4, members - 1)),
            dma((heads, 4)),
            dma((heads, 2)),
            dma((heads, 2)),
            dma((heads, 2)),
            dma((heads, 2)),
            dma((heads, 4, members - 1)),
            dma((heads, 4, members - 1)),
            dma((heads, 4)),
        ]
        + [pltpu.VMEM((3 * members, 2) + block, bf16)] * heads,
        compiler_params=pltpu.CompilerParams(collective_id=0, has_side_effects=True),
    )(pattern, live, query, key_in, value, grad_out)


def solution(mesh):
    rows = P(("groups", "seq", "head"), None)
    return jax.shard_map(
        functools.partial(body, mesh.shape["head"], mesh.shape["seq"]),
        mesh=mesh,
        in_specs=(rows, rows, rows, rows, P(), P()),
        out_specs=(rows, rows, rows, rows),
        check_vma=False,
    )
```

```python
import functools

import jax
import jax.numpy as jnp
from jax import lax
from jax.experimental import pallas as pl
from jax.experimental.pallas import tpu as pltpu
from jax.sharding import PartitionSpec as P

HEADS = 12
HEAD_DIM = 128
MESH = pl.DeviceIdType.MESH
NT = (((1,), (1,)), ((), ()))
NN = (((1,), (0,)), ((), ()))
TN = (((0,), (0,)), ((), ()))


def dot(a, b, dims):
    return lax.dot_general(a, b, dims, preferred_element_type=jnp.float32)


def flipped(index, bits, members):
    bit = 1
    while bit < members:
        if bits & bit:
            index = index + bit * (1 - 2 * lax.rem(lax.div(index, bit), 2))
        bit *= 2
    return index


def kernel(
    members, layers, pattern_in, live_in, query, key_in, value, grad_out,
    att_out, dq_out, dk_out, dv_out,
    qg, res, slots, own, gsend, grecv, total,
    pattern, live, table_sem, xin_send, xin_recv, xin_local, z_send, z_recv, zb_send, zb_recv,
    xb_send, xb_recv, xb_local, *kv,
):
    me = lax.axis_index("head")
    seq = lax.axis_index("seq")
    heads = HEADS // members
    nb = pattern.shape[0]
    first = seq * members
    scale = HEAD_DIM ** (-0.5)
    has_below = seq > 0
    has_above = seq < layers - 1
    below = jnp.maximum(seq - 1, 0)
    above = jnp.minimum(seq + 1, layers - 1)
    peers = [flipped(me, k, members) for k in range(members)]
    partners = peers[1:]

    def columns(owner, h):
        return pl.ds(pl.multiple_of((owner * heads + h) * HEAD_DIM, HEAD_DIM), HEAD_DIM)

    barrier = pltpu.get_barrier_semaphore()
    for p in partners:
        pl.semaphore_signal(barrier, inc=1, device_id={"head": p}, device_id_type=MESH)

    @pl.when(has_below)
    def _():
        pl.semaphore_signal(barrier, inc=1, device_id={"seq": below}, device_id_type=MESH)

    @pl.when(has_above)
    def _():
        pl.semaphore_signal(barrier, inc=1, device_id={"seq": above}, device_id_type=MESH)

    pl.semaphore_wait(
        barrier, members - 1 + has_below.astype(jnp.int32) + has_above.astype(jnp.int32)
    )

    sources = (key_in, value, query, grad_out)

    def landing(h, arr, tile):
        if arr < 2:
            return kv[h].at[members + tile, arr]
        return qg.at[h, tile, arr - 2]

    def x_in(h, arr, off):
        return pltpu.make_async_remote_copy(
            src_ref=sources[arr].at[:, columns(partners[off], h)],
            dst_ref=landing(h, arr, me),
            send_sem=xin_send.at[h, arr, off],
            recv_sem=xin_recv.at[h, arr, off],
            device_id={"head": partners[off]},
            device_id_type=MESH,
        )

    def x_own(h, arr):
        return pltpu.make_async_copy(
            sources[arr].at[:, columns(me, h)], landing(h, arr, me), xin_local.at[h, arr]
        )

    def x_in_wait(h, arrs, ks):
        for k in ks:
            for arr in arrs:
                if k == 0:
                    x_own(h, arr).wait()
                else:
                    x_in(h, arr, k - 1).wait_recv()

    def z_in(h, k, up):
        return pltpu.make_async_remote_copy(
            src_ref=kv[h].at[members + peers[k]],
            dst_ref=kv[h].at[peers[k] + (0 if up else 2 * members)],
            send_sem=z_send.at[h, k, up],
            recv_sem=z_recv.at[h, k, up],
            device_id={"seq": above if up else below},
            device_id_type=MESH,
        )

    def z_back(h, k, up):
        return pltpu.make_async_remote_copy(
            src_ref=gsend.at[h, up, peers[k]],
            dst_ref=grecv.at[h, up, peers[k]],
            send_sem=zb_send.at[h, k, up],
            recv_sem=zb_recv.at[h, k, up],
            device_id={"seq": above if up else below},
            device_id_type=MESH,
        )

    def z_start(make, h, ks):
        for up, there in ((1, has_above), (0, has_below)):
            @pl.when(there)
            def _():
                for k in ks:
                    make(h, k, up).start()

    def z_wait_recv(make, h, ks):
        for up, there in ((1, has_below), (0, has_above)):
            @pl.when(there)
            def _():
                for k in ks:
                    make(h, k, up).wait_recv()

    def z_wait_send(make, h, ks):
        for up, there in ((1, has_above), (0, has_below)):
            @pl.when(there)
            def _():
                for k in ks:
                    make(h, k, up).wait_send()

    results = (dk_out, dv_out, att_out, dq_out)

    def outgoing(h, arr, tile):
        if arr < 2:
            return total.at[h, tile, arr]
        return res.at[h, tile, arr - 2]

    def x_back(h, arr, off):
        return pltpu.make_async_remote_copy(
            src_ref=outgoing(h, arr, partners[off]),
            dst_ref=results[arr].at[:, columns(me, h)],
            send_sem=xb_send.at[h, arr, off],
            recv_sem=xb_recv.at[h, arr, off],
            device_id={"head": partners[off]},
            device_id_type=MESH,
        )

    def x_back_own(h, arr):
        return pltpu.make_async_copy(
            outgoing(h, arr, me), results[arr].at[:, columns(me, h)], xb_local.at[h, arr]
        )

    def x_back_start(h, arrs, ks):
        for k in ks:
            for arr in arrs:
                if k == 0:
                    x_back_own(h, arr).start()
                else:
                    x_back(h, arr, k - 1).start()

    def attend(h):
        def tile_step(a, carry):
            row = first + a
            ids = [
                jnp.clip(pattern[n, row] - first + members, 0, 3 * members - 1) for n in range(nb)
            ]
            bias = [jnp.where(live[n, row] > 0, 0.0, -jnp.inf) for n in range(nb)]
            q = qg[h, a, 0]
            g = qg[h, a, 1]
            scores = [dot(q, kv[h][ids[n], 0], NT) * scale + bias[n] for n in range(nb)]
            peak = functools.reduce(
                jnp.maximum, [jnp.max(s, axis=1, keepdims=True) for s in scores]
            )
            exps = [jnp.exp(s - peak) for s in scores]
            norm = 1.0 / sum(jnp.sum(e, axis=1, keepdims=True) for e in exps)
            weights = [e * norm for e in exps]
            low = [w.astype(jnp.bfloat16) for w in weights]
            res[h, a, 0] = sum(dot(low[n], kv[h][ids[n], 1], NN) for n in range(nb)).astype(
                jnp.bfloat16
            )
            wgrad = [dot(g, kv[h][ids[n], 1], NT) for n in range(nb)]
            delta = sum(
                jnp.sum(weights[n] * wgrad[n], axis=1, keepdims=True) for n in range(nb)
            )
            sgrad = [
                (weights[n] * (wgrad[n] - delta) * scale).astype(jnp.bfloat16)
                for n in range(nb)
            ]
            res[h, a, 1] = sum(dot(sgrad[n], kv[h][ids[n], 0], NN) for n in range(nb)).astype(
                jnp.bfloat16
            )
            for n in range(nb):
                slots[a * nb + n, 0] = dot(sgrad[n], q, TN)
                slots[a * nb + n, 1] = dot(low[n], g, TN)
            return carry

        lax.fori_loop(0, members, tile_step, 0)

    def gather_slots(j, which):
        terms = []
        for a in range(members):
            row = first + a
            index = jnp.int32(members * nb)
            for n in range(nb):
                hit = (pattern[n, row] - first + members == j) & (live[n, row] > 0)
                index = jnp.where(hit, a * nb + n, index)
            terms.append(index)
        return sum(slots[index, which] for index in terms)

    def spread(h):
        def outer(j, carry):
            for which in range(2):
                gsend[h, 0, j, which] = gather_slots(j, which).astype(jnp.bfloat16)
                gsend[h, 1, j, which] = gather_slots(j + 2 * members, which).astype(jnp.bfloat16)
            return carry

        lax.fori_loop(0, members, outer, 0)

        def inner(j, carry):
            for which in range(2):
                own[h, j, which] = gather_slots(j + members, which)
            return carry

        lax.fori_loop(0, members, inner, 0)

    def finish(h):
        for k in outward:
            tile = peers[k]
            z_wait_recv(z_back, h, (k,))

            @pl.when(has_below)
            def _():
                own[h, tile] += grecv[h, 1, tile].astype(jnp.float32)

            @pl.when(has_above)
            def _():
                own[h, tile] += grecv[h, 0, tile].astype(jnp.float32)

            total[h, tile] = own[h, tile].astype(jnp.bfloat16)
            x_back_start(h, (0, 1), (k,))

    everyone = tuple(range(members))
    near, far = everyone[:2], everyone[2:]
    outward = everyone[::-1]

    table_copies = [
        pltpu.make_async_copy(pattern_in, pattern, table_sem.at[0]),
        pltpu.make_async_copy(live_in, live, table_sem.at[1]),
    ]
    for copy in table_copies:
        copy.start()
    for h in range(heads):
        for arrs in ((0, 1), (2, 3)):
            for k in everyone:
                for arr in arrs:
                    if k == 0:
                        x_own(h, arr).start()
                    else:
                        x_in(h, arr, k - 1).start()

    slots[members * nb] = jnp.zeros(slots.shape[1:], slots.dtype)

    def feed(h, ks):
        x_in_wait(h, (0, 1), ks)
        z_start(z_in, h, ks)

    def work(h):
        x_in_wait(h, (2, 3), everyone)
        z_wait_recv(z_in, h, everyone)
        attend(h)
        x_back_start(h, (2, 3), outward)
        spread(h)

    ahead = [(h, ks) for h in range(heads) for ks in (near, far)]
    for h, ks in ahead[:5]:
        feed(h, ks)
    for copy in table_copies:
        copy.wait()
    for h in range(heads):
        work(h)
        if h == 0:
            for item in ahead[5:]:
                feed(*item)
        z_start(z_back, h, outward)
    for h in range(heads):
        finish(h)

    for h in range(heads):
        z_wait_send(z_in, h, everyone)
        z_wait_send(z_back, h, everyone)
        for arr in range(4):
            x_back_own(h, arr).wait()
            for off in range(members - 1):
                x_in(h, arr, off).wait_send()
                x_back(h, arr, off).wait_send()
                x_back(h, arr, off).wait_recv()


def place(*refs):
    count = (len(refs) - 2) // 3
    sources, outs, held = refs[:count], refs[count : 2 * count], refs[2 * count : 3 * count]
    in_sem, out_sem = refs[-2:]
    parts = 2
    rows = sources[0].shape[0] // parts
    pieces = [(i, part) for i in range(count) for part in range(parts)]

    def load(i, part):
        rng = pl.ds(part * rows, rows)
        return pltpu.make_async_copy(sources[i].at[rng], held[i].at[rng], in_sem.at[i, part])

    def store(i, part):
        rng = pl.ds(part * rows, rows)
        return pltpu.make_async_copy(held[i].at[rng], outs[i].at[rng], out_sem.at[i, part])

    for piece in pieces:
        load(*piece).start()
    for piece in pieces:
        load(*piece).wait()
        store(*piece).start()
    for piece in pieces:
        store(*piece).wait()


def body(members, layers, query, key_in, value, grad_out, pattern, live):
    pattern, live = pattern.T, live.T
    tile = query.shape[0]
    heads = HEADS // members
    nb = pattern.shape[0]
    dma = pltpu.SemaphoreType.DMA
    bf16 = jnp.bfloat16
    block = (tile, HEAD_DIM)
    results = pl.pallas_call(
        functools.partial(kernel, members, layers),
        out_shape=[jax.ShapeDtypeStruct(query.shape, bf16)] * 4,
        in_specs=[pl.BlockSpec(memory_space=pl.ANY)] * 6,
        out_specs=[pl.BlockSpec(memory_space=pl.ANY)] * 4,
        scratch_shapes=[
            pltpu.VMEM((heads, members, 2) + block, bf16),
            pltpu.VMEM((heads, members, 2) + block, bf16),
            pltpu.VMEM((members * nb + 1, 2) + block, jnp.float32),
            pltpu.VMEM((heads, members, 2) + block, jnp.float32),
            pltpu.VMEM((heads, 2, members, 2) + block, bf16),
            pltpu.VMEM((heads, 2, members, 2) + block, bf16),
            pltpu.VMEM((heads, members, 2) + block, bf16),
            pltpu.SMEM(pattern.shape, jnp.int32),
            pltpu.SMEM(live.shape, jnp.int32),
            dma((2,)),
            dma((heads, 4, members - 1)),
            dma((heads, 4, members - 1)),
            dma((heads, 4)),
            dma((heads, members, 2)),
            dma((heads, members, 2)),
            dma((heads, members, 2)),
            dma((heads, members, 2)),
            dma((heads, 4, members - 1)),
            dma((heads, 4, members - 1)),
            dma((heads, 4)),
        ]
        + [pltpu.VMEM((3 * members, 2) + block, bf16)] * heads,
        compiler_params=pltpu.CompilerParams(collective_id=0, has_side_effects=True),
    )(pattern, live, query, key_in, value, grad_out)
    count = len(results)
    return pl.pallas_call(
        place,
        out_shape=[jax.ShapeDtypeStruct(query.shape, bf16)] * count,
        in_specs=[pl.BlockSpec(memory_space=pl.ANY)] * count,
        out_specs=[pl.BlockSpec(memory_space=pl.ANY)] * count,
        scratch_shapes=[pltpu.VMEM(query.shape, bf16)] * count + [dma((count, 2))] * 2,
    )(*results)


def solution(mesh):
    rows = P(("groups", "seq", "head"), None)
    return jax.shard_map(
        functools.partial(body, mesh.shape["head"], mesh.shape["seq"]),
        mesh=mesh,
        in_specs=(rows, rows, rows, rows, P(), P()),
        out_specs=(rows, rows, rows, rows),
        check_vma=False,
    )
```

```python
import functools

import jax
import jax.numpy as jnp
from jax import lax
from jax.experimental import pallas as pl
from jax.experimental.pallas import tpu as pltpu
from jax.sharding import PartitionSpec as P

HEADS = 12
HEAD_DIM = 128
MESH = pl.DeviceIdType.MESH
NT = (((1,), (1,)), ((), ()))
NN = (((1,), (0,)), ((), ()))
TN = (((0,), (0,)), ((), ()))


def dot(a, b, dims):
    return lax.dot_general(a, b, dims, preferred_element_type=jnp.float32)


def flipped(index, bits, members):
    bit = 1
    while bit < members:
        if bits & bit:
            index = index + bit * (1 - 2 * lax.rem(lax.div(index, bit), 2))
        bit *= 2
    return index


def kernel(
    members, layers, pattern_in, live_in, query, key_in, value, grad_out,
    att_out, dq_out, dk_out, dv_out,
    qg, res, slots, own, gsend, grecv, total,
    pattern, live, table_sem, xin_send, xin_recv, xin_local, z_send, z_recv, zb_send, zb_recv,
    xb_send, xb_recv, xb_local, *kv,
):
    me = lax.axis_index("head")
    seq = lax.axis_index("seq")
    heads = HEADS // members
    nb = pattern.shape[0]
    first = seq * members
    scale = HEAD_DIM ** (-0.5)
    has_below = seq > 0
    has_above = seq < layers - 1
    below = jnp.maximum(seq - 1, 0)
    above = jnp.minimum(seq + 1, layers - 1)
    peers = [flipped(me, k, members) for k in range(members)]
    partners = peers[1:]

    def columns(owner, h):
        return pl.ds(pl.multiple_of((owner * heads + h) * HEAD_DIM, HEAD_DIM), HEAD_DIM)

    sources = (key_in, value, query, grad_out)

    def landing(h, arr, tile):
        if arr < 2:
            return kv[h].at[members + tile, arr]
        return qg.at[h, tile, arr - 2]

    def x_in(h, arr, off):
        return pltpu.make_async_remote_copy(
            src_ref=sources[arr].at[:, columns(partners[off], h)],
            dst_ref=landing(h, arr, me),
            send_sem=xin_send.at[h, arr, off],
            recv_sem=xin_recv.at[h, arr, off],
            device_id={"head": partners[off]},
            device_id_type=MESH,
        )

    def x_own(h, arr):
        return pltpu.make_async_copy(
            sources[arr].at[:, columns(me, h)], landing(h, arr, me), xin_local.at[h, arr]
        )

    def x_in_wait(h, arrs, ks):
        for k in ks:
            for arr in arrs:
                if k == 0:
                    x_own(h, arr).wait()
                else:
                    x_in(h, arr, k - 1).wait_recv()

    def z_in(h, k, up):
        return pltpu.make_async_remote_copy(
            src_ref=kv[h].at[members + peers[k]],
            dst_ref=kv[h].at[peers[k] + (0 if up else 2 * members)],
            send_sem=z_send.at[h, k, up],
            recv_sem=z_recv.at[h, k, up],
            device_id={"seq": above if up else below},
            device_id_type=MESH,
        )

    def z_back(h, k, up):
        return pltpu.make_async_remote_copy(
            src_ref=gsend.at[h, up, peers[k]],
            dst_ref=grecv.at[h, up, peers[k]],
            send_sem=zb_send.at[h, k, up],
            recv_sem=zb_recv.at[h, k, up],
            device_id={"seq": above if up else below},
            device_id_type=MESH,
        )

    def z_start(make, h, ks):
        for up, there in ((1, has_above), (0, has_below)):
            @pl.when(there)
            def _():
                for k in ks:
                    make(h, k, up).start()

    def z_wait_recv(make, h, ks):
        for up, there in ((1, has_below), (0, has_above)):
            @pl.when(there)
            def _():
                for k in ks:
                    make(h, k, up).wait_recv()

    def z_wait_send(make, h, ks):
        for up, there in ((1, has_above), (0, has_below)):
            @pl.when(there)
            def _():
                for k in ks:
                    make(h, k, up).wait_send()

    results = (dk_out, dv_out, att_out, dq_out)

    def outgoing(h, arr, tile):
        if arr < 2:
            return total.at[h, tile, arr]
        return res.at[h, tile, arr - 2]

    def x_back(h, arr, off):
        return pltpu.make_async_remote_copy(
            src_ref=outgoing(h, arr, partners[off]),
            dst_ref=results[arr].at[:, columns(me, h)],
            send_sem=xb_send.at[h, arr, off],
            recv_sem=xb_recv.at[h, arr, off],
            device_id={"head": partners[off]},
            device_id_type=MESH,
        )

    def x_back_own(h, arr):
        return pltpu.make_async_copy(
            outgoing(h, arr, me), results[arr].at[:, columns(me, h)], xb_local.at[h, arr]
        )

    def x_back_start(h, arrs, ks):
        for k in ks:
            for arr in arrs:
                if k == 0:
                    x_back_own(h, arr).start()
                else:
                    x_back(h, arr, k - 1).start()

    def attend(h):
        def tile_step(a, carry):
            row = first + a
            ids = [
                jnp.clip(pattern[n, row] - first + members, 0, 3 * members - 1) for n in range(nb)
            ]
            bias = [jnp.where(live[n, row] > 0, 0.0, -jnp.inf) for n in range(nb)]
            q = qg[h, a, 0]
            g = qg[h, a, 1]
            scores = [dot(q, kv[h][ids[n], 0], NT) * scale + bias[n] for n in range(nb)]
            peak = functools.reduce(
                jnp.maximum, [jnp.max(s, axis=1, keepdims=True) for s in scores]
            )
            exps = [jnp.exp(s - peak) for s in scores]
            norm = 1.0 / sum(jnp.sum(e, axis=1, keepdims=True) for e in exps)
            weights = [e * norm for e in exps]
            low = [w.astype(jnp.bfloat16) for w in weights]
            res[h, a, 0] = sum(dot(low[n], kv[h][ids[n], 1], NN) for n in range(nb)).astype(
                jnp.bfloat16
            )
            wgrad = [dot(g, kv[h][ids[n], 1], NT) for n in range(nb)]
            delta = sum(
                jnp.sum(weights[n] * wgrad[n], axis=1, keepdims=True) for n in range(nb)
            )
            sgrad = [
                (weights[n] * (wgrad[n] - delta) * scale).astype(jnp.bfloat16)
                for n in range(nb)
            ]
            res[h, a, 1] = sum(dot(sgrad[n], kv[h][ids[n], 0], NN) for n in range(nb)).astype(
                jnp.bfloat16
            )
            for n in range(nb):
                slots[a * nb + n, 0] = dot(sgrad[n], q, TN)
                slots[a * nb + n, 1] = dot(low[n], g, TN)
            return carry

        lax.fori_loop(0, members, tile_step, 0)

    def gather_slots(j, which):
        terms = []
        for a in range(members):
            row = first + a
            index = jnp.int32(members * nb)
            for n in range(nb):
                hit = (pattern[n, row] - first + members == j) & (live[n, row] > 0)
                index = jnp.where(hit, a * nb + n, index)
            terms.append(index)
        return sum(slots[index, which] for index in terms)

    def spread(h):
        def outer(j, carry):
            for which in range(2):
                gsend[h, 0, j, which] = gather_slots(j, which).astype(jnp.bfloat16)
                gsend[h, 1, j, which] = gather_slots(j + 2 * members, which).astype(jnp.bfloat16)
            return carry

        lax.fori_loop(0, members, outer, 0)

        def inner(j, carry):
            for which in range(2):
                own[h, j, which] = gather_slots(j + members, which)
            return carry

        lax.fori_loop(0, members, inner, 0)

    def finish(h):
        for k in outward:
            tile = peers[k]
            z_wait_recv(z_back, h, (k,))

            @pl.when(has_below)
            def _():
                own[h, tile] += grecv[h, 1, tile].astype(jnp.float32)

            @pl.when(has_above)
            def _():
                own[h, tile] += grecv[h, 0, tile].astype(jnp.float32)

            total[h, tile] = own[h, tile].astype(jnp.bfloat16)
            x_back_start(h, (0, 1), (k,))

    everyone = tuple(range(members))
    near, far = everyone[:2], everyone[2:]
    outward = everyone[::-1]
    partner_ks = everyone[1:]

    table_copies = [
        pltpu.make_async_copy(pattern_in, pattern, table_sem.at[0]),
        pltpu.make_async_copy(live_in, live, table_sem.at[1]),
    ]
    for h in range(heads):
        for arr in range(4):
            x_own(h, arr).start()
    for copy in table_copies:
        copy.start()

    barrier = pltpu.get_barrier_semaphore()
    for p in partners:
        pl.semaphore_signal(barrier, inc=1, device_id={"head": p}, device_id_type=MESH)

    @pl.when(has_below)
    def _():
        pl.semaphore_signal(barrier, inc=1, device_id={"seq": below}, device_id_type=MESH)

    @pl.when(has_above)
    def _():
        pl.semaphore_signal(barrier, inc=1, device_id={"seq": above}, device_id_type=MESH)

    pl.semaphore_wait(
        barrier, members - 1 + has_below.astype(jnp.int32) + has_above.astype(jnp.int32)
    )

    def feed(h, ks):
        x_in_wait(h, (0, 1), ks)
        z_start(z_in, h, ks)

    feed(0, near[:1])
    for h in range(heads):
        for arrs in ((0, 1), (2, 3)):
            for k in partner_ks:
                for arr in arrs:
                    x_in(h, arr, k - 1).start()

    slots[members * nb] = jnp.zeros(slots.shape[1:], slots.dtype)

    def work(h):
        x_in_wait(h, (2, 3), everyone)
        z_wait_recv(z_in, h, everyone)
        attend(h)
        x_back_start(h, (2, 3), outward)
        spread(h)

    ahead = [(h, ks) for h in range(heads) for ks in (near, far)]
    ahead[0] = (0, near[1:])
    for h, ks in ahead[:5]:
        feed(h, ks)
    for copy in table_copies:
        copy.wait()
    for h in range(heads):
        work(h)
        if h == 0:
            for item in ahead[5:]:
                feed(*item)
        z_start(z_back, h, outward)
    for h in range(heads):
        finish(h)

    for h in range(heads):
        z_wait_send(z_in, h, everyone)
        z_wait_send(z_back, h, everyone)
        for arr in range(4):
            x_back_own(h, arr).wait()
            for off in range(members - 1):
                x_in(h, arr, off).wait_send()
                x_back(h, arr, off).wait_send()
                x_back(h, arr, off).wait_recv()


def place(*refs):
    count = (len(refs) - 2) // 3
    sources, outs, held = refs[:count], refs[count : 2 * count], refs[2 * count : 3 * count]
    in_sem, out_sem = refs[-2:]
    parts = 2
    rows = sources[0].shape[0] // parts
    pieces = [(i, part) for i in range(count) for part in range(parts)]

    def load(i, part):
        rng = pl.ds(part * rows, rows)
        return pltpu.make_async_copy(sources[i].at[rng], held[i].at[rng], in_sem.at[i, part])

    def store(i, part):
        rng = pl.ds(part * rows, rows)
        return pltpu.make_async_copy(held[i].at[rng], outs[i].at[rng], out_sem.at[i, part])

    for piece in pieces:
        load(*piece).start()
    for piece in pieces:
        load(*piece).wait()
        store(*piece).start()
    for piece in pieces:
        store(*piece).wait()


def body(members, layers, query, key_in, value, grad_out, pattern, live):
    pattern, live = pattern.T, live.T
    tile = query.shape[0]
    heads = HEADS // members
    nb = pattern.shape[0]
    dma = pltpu.SemaphoreType.DMA
    bf16 = jnp.bfloat16
    block = (tile, HEAD_DIM)
    results = pl.pallas_call(
        functools.partial(kernel, members, layers),
        out_shape=[jax.ShapeDtypeStruct(query.shape, bf16)] * 4,
        in_specs=[pl.BlockSpec(memory_space=pl.ANY)] * 6,
        out_specs=[pl.BlockSpec(memory_space=pl.ANY)] * 4,
        scratch_shapes=[
            pltpu.VMEM((heads, members, 2) + block, bf16),
            pltpu.VMEM((heads, members, 2) + block, bf16),
            pltpu.VMEM((members * nb + 1, 2) + block, jnp.float32),
            pltpu.VMEM((heads, members, 2) + block, jnp.float32),
            pltpu.VMEM((heads, 2, members, 2) + block, bf16),
            pltpu.VMEM((heads, 2, members, 2) + block, bf16),
            pltpu.VMEM((heads, members, 2) + block, bf16),
            pltpu.SMEM(pattern.shape, jnp.int32),
            pltpu.SMEM(live.shape, jnp.int32),
            dma((2,)),
            dma((heads, 4, members - 1)),
            dma((heads, 4, members - 1)),
            dma((heads, 4)),
            dma((heads, members, 2)),
            dma((heads, members, 2)),
            dma((heads, members, 2)),
            dma((heads, members, 2)),
            dma((heads, 4, members - 1)),
            dma((heads, 4, members - 1)),
            dma((heads, 4)),
        ]
        + [pltpu.VMEM((3 * members, 2) + block, bf16)] * heads,
        compiler_params=pltpu.CompilerParams(collective_id=0, has_side_effects=True),
    )(pattern, live, query, key_in, value, grad_out)
    count = len(results)
    return pl.pallas_call(
        place,
        out_shape=[jax.ShapeDtypeStruct(query.shape, bf16)] * count,
        in_specs=[pl.BlockSpec(memory_space=pl.ANY)] * count,
        out_specs=[pl.BlockSpec(memory_space=pl.ANY)] * count,
        scratch_shapes=[pltpu.VMEM(query.shape, bf16)] * count + [dma((count, 2))] * 2,
    )(*results)


def solution(mesh):
    rows = P(("groups", "seq", "head"), None)
    return jax.shard_map(
        functools.partial(body, mesh.shape["head"], mesh.shape["seq"]),
        mesh=mesh,
        in_specs=(rows, rows, rows, rows, P(), P()),
        out_specs=(rows, rows, rows, rows),
        check_vma=False,
    )
```

```python
import functools

import jax
import jax.numpy as jnp
from jax import lax
from jax.experimental import pallas as pl
from jax.experimental.pallas import tpu as pltpu
from jax.sharding import PartitionSpec as P

HEADS = 12
HEAD_DIM = 128
MESH = pl.DeviceIdType.MESH
NT = (((1,), (1,)), ((), ()))
NN = (((1,), (0,)), ((), ()))
TN = (((0,), (0,)), ((), ()))


def dot(a, b, dims):
    return lax.dot_general(a, b, dims, preferred_element_type=jnp.float32)


def flipped(index, bits, members):
    bit = 1
    while bit < members:
        if bits & bit:
            index = index + bit * (1 - 2 * lax.rem(lax.div(index, bit), 2))
        bit *= 2
    return index


def kernel(
    members, layers, pattern_in, live_in, query, key_in, value, grad_out,
    att_out, dq_out, dk_out, dv_out,
    qg, res, slots, own, gsend, grecv, total,
    pattern, live, table_sem, xin_send, xin_recv, xin_local, z_send, z_recv, zb_send, zb_recv,
    xb_send, xb_recv, xb_local, *kv,
):
    me = lax.axis_index("head")
    seq = lax.axis_index("seq")
    heads = HEADS // members
    nb = pattern.shape[0]
    first = seq * members
    scale = HEAD_DIM ** (-0.5)
    has_below = seq > 0
    has_above = seq < layers - 1
    below = jnp.maximum(seq - 1, 0)
    above = jnp.minimum(seq + 1, layers - 1)
    peers = [flipped(me, k, members) for k in range(members)]
    partners = peers[1:]

    def columns(owner, h):
        return pl.ds(pl.multiple_of((owner * heads + h) * HEAD_DIM, HEAD_DIM), HEAD_DIM)

    sources = (key_in, value, query, grad_out)

    def landing(h, arr, tile):
        if arr < 2:
            return kv[h].at[members + tile, arr]
        return qg.at[h, tile, arr - 2]

    def x_in(h, arr, off):
        return pltpu.make_async_remote_copy(
            src_ref=sources[arr].at[:, columns(partners[off], h)],
            dst_ref=landing(h, arr, me),
            send_sem=xin_send.at[h, arr, off],
            recv_sem=xin_recv.at[h, arr, off],
            device_id={"head": partners[off]},
            device_id_type=MESH,
        )

    def x_own(h, arr):
        return pltpu.make_async_copy(
            sources[arr].at[:, columns(me, h)], landing(h, arr, me), xin_local.at[h, arr]
        )

    def x_in_wait(h, arrs, ks):
        for k in ks:
            for arr in arrs:
                if k == 0:
                    x_own(h, arr).wait()
                else:
                    x_in(h, arr, k - 1).wait_recv()

    def z_in(h, k, up):
        return pltpu.make_async_remote_copy(
            src_ref=kv[h].at[members + peers[k]],
            dst_ref=kv[h].at[peers[k] + (0 if up else 2 * members)],
            send_sem=z_send.at[h, k, up],
            recv_sem=z_recv.at[h, k, up],
            device_id={"seq": above if up else below},
            device_id_type=MESH,
        )

    def z_back(h, k, up):
        return pltpu.make_async_remote_copy(
            src_ref=gsend.at[h, up, peers[k]],
            dst_ref=grecv.at[h, up, peers[k]],
            send_sem=zb_send.at[h, k, up],
            recv_sem=zb_recv.at[h, k, up],
            device_id={"seq": above if up else below},
            device_id_type=MESH,
        )

    def z_start(make, h, ks):
        for up, there in ((1, has_above), (0, has_below)):
            @pl.when(there)
            def _():
                for k in ks:
                    make(h, k, up).start()

    def z_wait_recv(make, h, ks):
        for up, there in ((1, has_below), (0, has_above)):
            @pl.when(there)
            def _():
                for k in ks:
                    make(h, k, up).wait_recv()

    def z_wait_send(make, h, ks):
        for up, there in ((1, has_above), (0, has_below)):
            @pl.when(there)
            def _():
                for k in ks:
                    make(h, k, up).wait_send()

    results = (dk_out, dv_out, att_out, dq_out)

    def outgoing(h, arr, tile):
        if arr < 2:
            return total.at[h, tile, arr]
        return res.at[h, tile, arr - 2]

    def x_back(h, arr, off):
        return pltpu.make_async_remote_copy(
            src_ref=outgoing(h, arr, partners[off]),
            dst_ref=results[arr].at[:, columns(me, h)],
            send_sem=xb_send.at[h, arr, off],
            recv_sem=xb_recv.at[h, arr, off],
            device_id={"head": partners[off]},
            device_id_type=MESH,
        )

    def x_back_own(h, arr):
        return pltpu.make_async_copy(
            outgoing(h, arr, me), results[arr].at[:, columns(me, h)], xb_local.at[h, arr]
        )

    def x_back_start(h, arrs, ks):
        for k in ks:
            for arr in arrs:
                if k == 0:
                    x_back_own(h, arr).start()
                else:
                    x_back(h, arr, k - 1).start()

    def attend(h):
        def tile_step(a, carry):
            row = first + a
            ids = [
                jnp.clip(pattern[n, row] - first + members, 0, 3 * members - 1) for n in range(nb)
            ]
            bias = [jnp.where(live[n, row] > 0, 0.0, -jnp.inf) for n in range(nb)]
            q = qg[h, a, 0]
            g = qg[h, a, 1]
            scores = [dot(q, kv[h][ids[n], 0], NT) * scale + bias[n] for n in range(nb)]
            peak = functools.reduce(
                jnp.maximum, [jnp.max(s, axis=1, keepdims=True) for s in scores]
            )
            exps = [jnp.exp(s - peak) for s in scores]
            norm = 1.0 / sum(jnp.sum(e, axis=1, keepdims=True) for e in exps)
            weights = [e * norm for e in exps]
            low = [w.astype(jnp.bfloat16) for w in weights]
            res[h, a, 0] = sum(dot(low[n], kv[h][ids[n], 1], NN) for n in range(nb)).astype(
                jnp.bfloat16
            )
            wgrad = [dot(g, kv[h][ids[n], 1], NT) for n in range(nb)]
            delta = sum(
                jnp.sum(weights[n] * wgrad[n], axis=1, keepdims=True) for n in range(nb)
            )
            sgrad = [
                (weights[n] * (wgrad[n] - delta) * scale).astype(jnp.bfloat16)
                for n in range(nb)
            ]
            res[h, a, 1] = sum(dot(sgrad[n], kv[h][ids[n], 0], NN) for n in range(nb)).astype(
                jnp.bfloat16
            )
            for n in range(nb):
                slots[a * nb + n, 0] = dot(sgrad[n], q, TN)
                slots[a * nb + n, 1] = dot(low[n], g, TN)
            return carry

        lax.fori_loop(0, members, tile_step, 0)

    def gather_slots(j, which):
        terms = []
        for a in range(members):
            row = first + a
            index = jnp.int32(members * nb)
            for n in range(nb):
                hit = (pattern[n, row] - first + members == j) & (live[n, row] > 0)
                index = jnp.where(hit, a * nb + n, index)
            terms.append(index)
        return sum(slots[index, which] for index in terms)

    def spread(h):
        def outer(j, carry):
            for which in range(2):
                gsend[h, 0, j, which] = gather_slots(j, which).astype(jnp.bfloat16)
                gsend[h, 1, j, which] = gather_slots(j + 2 * members, which).astype(jnp.bfloat16)
            return carry

        lax.fori_loop(0, members, outer, 0)

        def inner(j, carry):
            for which in range(2):
                own[h, j, which] = gather_slots(j + members, which)
            return carry

        lax.fori_loop(0, members, inner, 0)

    def finish(h):
        for k in outward:
            tile = peers[k]
            z_wait_recv(z_back, h, (k,))

            @pl.when(has_below)
            def _():
                own[h, tile] += grecv[h, 1, tile].astype(jnp.float32)

            @pl.when(has_above)
            def _():
                own[h, tile] += grecv[h, 0, tile].astype(jnp.float32)

            total[h, tile] = own[h, tile].astype(jnp.bfloat16)
            x_back_start(h, (0, 1), (k,))

    everyone = tuple(range(members))
    near, far = everyone[:2], everyone[2:]
    outward = everyone[::-1]
    partner_ks = everyone[1:]

    table_copies = [
        pltpu.make_async_copy(pattern_in, pattern, table_sem.at[0]),
        pltpu.make_async_copy(live_in, live, table_sem.at[1]),
    ]
    for h in range(heads):
        for arr in range(4):
            x_own(h, arr).start()
    for copy in table_copies:
        copy.start()

    barrier = pltpu.get_barrier_semaphore()
    for p in partners:
        pl.semaphore_signal(barrier, inc=1, device_id={"head": p}, device_id_type=MESH)

    @pl.when(has_below)
    def _():
        pl.semaphore_signal(barrier, inc=1, device_id={"seq": below}, device_id_type=MESH)

    @pl.when(has_above)
    def _():
        pl.semaphore_signal(barrier, inc=1, device_id={"seq": above}, device_id_type=MESH)

    pl.semaphore_wait(
        barrier, members - 1 + has_below.astype(jnp.int32) + has_above.astype(jnp.int32)
    )

    def feed(h, ks):
        x_in_wait(h, (0, 1), ks)
        z_start(z_in, h, ks)

    feed(0, near[:1])
    for h in range(heads):
        for arrs in ((0, 1), (2, 3)):
            for k in partner_ks:
                for arr in arrs:
                    x_in(h, arr, k - 1).start()

    slots[members * nb] = jnp.zeros(slots.shape[1:], slots.dtype)

    def work(h):
        x_in_wait(h, (2, 3), everyone)
        z_wait_recv(z_in, h, everyone)
        attend(h)
        x_back_start(h, (2, 3), outward)
        spread(h)

    ahead = [(h, ks) for h in range(heads) for ks in (near, far)]
    ahead[0] = (0, near[1:])
    for h, ks in ahead[:5]:
        feed(h, ks)
    for copy in table_copies:
        copy.wait()
    for h in range(heads):
        work(h)
        if h == 0:
            for item in ahead[5:]:
                feed(*item)
        z_start(z_back, h, outward)
    for h in range(heads):
        finish(h)

    for h in range(heads):
        z_wait_send(z_in, h, everyone)
        z_wait_send(z_back, h, everyone)
        for arr in range(4):
            x_back_own(h, arr).wait()
            for off in range(members - 1):
                x_in(h, arr, off).wait_send()
                x_back(h, arr, off).wait_send()
                x_back(h, arr, off).wait_recv()


def place(*refs):
    count = len(refs) // 2
    sems = refs[-1]
    copies = [
        pltpu.make_async_copy(refs[i], refs[count + i], sems.at[i]) for i in range(count)
    ]
    for copy in copies:
        copy.start()
    for copy in copies:
        copy.wait()


def body(members, layers, query, key_in, value, grad_out, pattern, live):
    pattern, live = pattern.T, live.T
    tile = query.shape[0]
    heads = HEADS // members
    nb = pattern.shape[0]
    dma = pltpu.SemaphoreType.DMA
    bf16 = jnp.bfloat16
    block = (tile, HEAD_DIM)
    results = pl.pallas_call(
        functools.partial(kernel, members, layers),
        out_shape=[jax.ShapeDtypeStruct(query.shape, bf16)] * 4,
        in_specs=[pl.BlockSpec(memory_space=pl.ANY)] * 6,
        out_specs=[pl.BlockSpec(memory_space=pl.ANY)] * 4,
        scratch_shapes=[
            pltpu.VMEM((heads, members, 2) + block, bf16),
            pltpu.VMEM((heads, members, 2) + block, bf16),
            pltpu.VMEM((members * nb + 1, 2) + block, jnp.float32),
            pltpu.VMEM((heads, members, 2) + block, jnp.float32),
            pltpu.VMEM((heads, 2, members, 2) + block, bf16),
            pltpu.VMEM((heads, 2, members, 2) + block, bf16),
            pltpu.VMEM((heads, members, 2) + block, bf16),
            pltpu.SMEM(pattern.shape, jnp.int32),
            pltpu.SMEM(live.shape, jnp.int32),
            dma((2,)),
            dma((heads, 4, members - 1)),
            dma((heads, 4, members - 1)),
            dma((heads, 4)),
            dma((heads, members, 2)),
            dma((heads, members, 2)),
            dma((heads, members, 2)),
            dma((heads, members, 2)),
            dma((heads, 4, members - 1)),
            dma((heads, 4, members - 1)),
            dma((heads, 4)),
        ]
        + [pltpu.VMEM((3 * members, 2) + block, bf16)] * heads,
        compiler_params=pltpu.CompilerParams(collective_id=0, has_side_effects=True, vmem_limit_bytes=40 * 2**20),
    )(pattern, live, query, key_in, value, grad_out)
    count = len(results)
    return pl.pallas_call(
        place,
        out_shape=[jax.ShapeDtypeStruct(query.shape, bf16)] * count,
        in_specs=[pl.BlockSpec(memory_space=pl.ANY)] * count,
        out_specs=[pl.BlockSpec(memory_space=pl.ANY)] * count,
        scratch_shapes=[dma((count,))],
        compiler_params=pltpu.CompilerParams(vmem_limit_bytes=8 * 2**20),
    )(*results)


def solution(mesh):
    rows = P(("groups", "seq", "head"), None)
    return jax.shard_map(
        functools.partial(body, mesh.shape["head"], mesh.shape["seq"]),
        mesh=mesh,
        in_specs=(rows, rows, rows, rows, P(), P()),
        out_specs=(rows, rows, rows, rows),
        check_vma=False,
    )
```
